32 devices in a mesh: dp: 8 (over y, x, core), ctx: 4 (over z).
Axes of the slice: x: 2, y: 2, z: 4, core: 2. Of those that a mesh axis runs over, the one named last changes fastest.
Arguments:
- inputs: bfloat16 [4096, 8192], P('ctx', 'dp'), may hold values from -6 to 6
- cotangent: bfloat16 [4096, 8192], P('ctx', 'dp'), may hold values from -6 to 6
- residue: float32 [8192], P('dp'), may hold values from -0.6 to 0.6
- decay: float32 [8192], P('dp'), may hold values from 7.324219e-05 to 0.05
- skip_gain: float32 [8192], P('dp'), may hold values from -4 to 4
- band_blocks: int32 [8, 4], P('dp'), may hold values from 0 to 3, each once within a row
Outputs:
- layer_out: bfloat16 [4096, 8192], P('ctx', 'dp')
- input_grad: bfloat16 [4096, 8192], P('ctx', 'dp')
- skip_grad: float32 [8192], P(('dp', 'ctx'))
- residue_grad: float32 [8192], P(('dp', 'ctx'))
- decay_grad: float32 [8192], P(('dp', 'ctx'))
The draws below stay inside these ranges and needn't reach their ends.
Inputs may be any that keep to these rules, and one draw needn't show every extreme that they name: Each row of band_blocks holds each of 0 to 3 exactly once.
All inputs are finite; a program needn't handle non-finite values.
Results may differ from the reference program's by a relative error of at most 0.0019.
Values may be sent and summed in bfloat16 or wider, within the bound.
A program may use at most 128 MiB of HBM per device.

```python
import math
import jax
import jax.numpy as jnp
from jax import lax

C = 8192
TOK_DEV = 1024
CG = 256
CD = 1024
SEQ = 4096
N_DP = 8
N_CTX = 4


def steps_of(own_key, extent, shards, smallest, largest):
    gain = 1.0
    for axis_at, shards_of in shards:
        draws = jax.random.uniform(jax.random.fold_in(jax.random.fold_in(own_key, 6), axis_at), (shards_of,), jnp.float32, smallest / len(shards), largest / len(shards))
        gain = gain * jnp.repeat(jnp.exp(draws), extent[axis_at] // shards_of).reshape((-1,) + (1,) * (len(extent) - 1 - axis_at))
    return gain


def centred(own_key, dims, spread, bound, split=(), kind=jnp.bfloat16):
    drawn = spread * jax.random.normal(own_key, dims, jnp.float32)
    if split:
        drawn = drawn * steps_of(own_key, dims, split, -0.22, 0.18)
    return jnp.clip(drawn, -bound, bound).astype(kind)


def setup_inputs(seed: int = 0) -> dict:
    streams_of = jax.random.split(jax.random.key(seed), 7)
    return {
        "inputs": centred(streams_of[0], (SEQ, C), 1.0, 6.0, ((0, 4), (1, 8))),
        "cotangent": centred(streams_of[1], (SEQ, C), 1.0, 6.0, ((0, 4), (1, 8))),
        "residue": centred(streams_of[2], (C,), 0.15, 0.6, ((0, 8),), jnp.float32),
        "decay": jnp.clip(jnp.exp(math.log(0.05) - 6.5260067 * jax.random.uniform(streams_of[3], (C,), jnp.float32) ** steps_of(streams_of[3], (C,), ((0, 8),), -0.2, 0.2)), 7.324219041038305e-05, 0.05),
        "skip_gain": centred(streams_of[4], (C,), 1.0, 4.0, ((0, 8),), jnp.float32),
        "band_blocks": jax.vmap(lambda own: jax.random.permutation(own, N_CTX))(jax.random.split(streams_of[5], N_DP)).reshape((N_DP, N_CTX)).astype(jnp.int32),
    }


def compose(earlier_pair, later_pair):
    return (earlier_pair[0] * later_pair[0], earlier_pair[1] * later_pair[0] + later_pair[1])

def causal_sum(values, decay_rate):
    factors = jnp.broadcast_to(jnp.exp(-decay_rate)[None, :], values.shape)
    return lax.associative_scan(compose, (factors, values))[1]

def filtered(values, decay_rate, lengths):
    summed = causal_sum(values, decay_rate)
    shifted_index = jnp.arange(SEQ, dtype=jnp.int32)[:, None] - lengths[None, :]
    earlier = jnp.take_along_axis(summed, jnp.maximum(shifted_index, 0).astype(jnp.int32), axis=0)
    earlier = jnp.where(shifted_index >= 0, earlier, jnp.zeros_like(earlier))
    return summed - jnp.exp(-decay_rate * lengths.astype(jnp.float32))[None, :] * earlier

def reference(inputs, cotangent, residue, decay, skip_gain, band_blocks):
    lengths = jnp.repeat(((band_blocks.reshape(-1) + 1) * TOK_DEV).astype(jnp.int32), CG, total_repeat_length=C)

    def layer(values, res_arg, decay_arg, skip_arg, slab_lengths):
        return skip_arg[None, :] * values + res_arg[None, :] * filtered(values, decay_arg, slab_lengths)

    def one_slab(pack):
        values = pack[0].astype(jnp.float32)
        upstream = pack[1].astype(jnp.float32)
        res_s, dec_s, skip_s, len_s = (pack[2], pack[3], pack[4], pack[5])

        def local_layer(v, r, d, k):
            return layer(v, r, d, k, len_s)
        result, pullback = jax.vjp(local_layer, values, res_s, dec_s, skip_s)
        grad_in, grad_res, grad_decay, grad_skip = pullback(upstream)
        stacked = jnp.stack([grad_skip, grad_res, grad_decay * dec_s])
        return (result.astype(jnp.bfloat16), grad_in.astype(jnp.bfloat16), stacked)
    slab_in = jnp.transpose(inputs.reshape(SEQ, N_DP, CD), (1, 0, 2))
    slab_ct = jnp.transpose(cotangent.reshape(SEQ, N_DP, CD), (1, 0, 2))
    outputs, grads_in, stacked = lax.map(one_slab, (slab_in, slab_ct, residue.reshape(N_DP, CD), decay.reshape(N_DP, CD), skip_gain.reshape(N_DP, CD), lengths.reshape(N_DP, CD)))
    outputs = jnp.transpose(outputs, (1, 0, 2)).reshape(SEQ, C)
    grads_in = jnp.transpose(grads_in, (1, 0, 2)).reshape(SEQ, C)
    grads = jnp.transpose(stacked, (1, 0, 2)).reshape(3, C)
    return (outputs, grads_in, grads[0], grads[1], grads[2])
```

```python
import functools
import jax
import jax.numpy as jnp
from jax import lax
from jax.experimental import pallas as pl
from jax.experimental.pallas import tpu as pltpu
from jax.sharding import PartitionSpec as P


def prefix(value, axis, join, neutral, backward):
    count, mine = (lax.axis_size(axis), lax.axis_index(axis))
    pieces = jax.tree.map(lambda part: lax.all_gather(part, axis), value)
    if backward:
        pieces = jax.tree.map(lambda part: part[::-1], pieces)
        mine = count - 1 - mine
    total = jax.tree.map(
        lambda part, zero: jnp.full_like(part, 0) + jnp.asarray(zero, part.dtype), value, neutral
    )

    def turn(position, total):
        longer = join(total, jax.tree.map(lambda part: part[position], pieces))
        return jax.tree.map(lambda new, old: jnp.where(position < mine, new, old), longer, total)

    return lax.fori_loop(0, count - 1, turn, total)


def compose(earlier_pair, later_pair):
    return (earlier_pair[0] * later_pair[0], earlier_pair[1] * later_pair[0] + later_pair[1])


def chain_step(earlier_pair, later_pair):
    return (earlier_pair[0] * later_pair[1] + later_pair[0], earlier_pair[1] * later_pair[1])


def local_scan(values, decay_rate, backward):
    factors = jnp.broadcast_to(jnp.exp(-decay_rate)[None, :], values.shape)
    return lax.associative_scan(compose, (factors, values), reverse=backward)[1]


def slot_groups(bands, ctx_rank, direction):
    group_count = bands.shape[0]
    slot_index = jnp.arange(group_count, dtype=jnp.int32)
    distance = (slot_index - ctx_rank) * direction
    matches = bands[None, :] + 1 == distance[:, None]
    return jnp.sum(jnp.where(matches, slot_index[None, :], 0), axis=1)


def outgoing(values, slot_group, group_count, group_width):
    shaped = values.reshape(values.shape[0], group_count, group_width)
    return jnp.take(shaped, slot_group, axis=1)


def incoming(received, source, in_range):
    picked = jnp.take(received, source, axis=1)
    picked = jnp.where(in_range[None, :, None], picked, jnp.zeros((), picked.dtype))
    return picked.reshape(picked.shape[0], -1)


def body(inputs, cotangent, residue, decay, skip_gain, band_blocks):
    values = inputs.astype(jnp.float32)
    upstream = cotangent.astype(jnp.float32)
    bands = band_blocks[0]
    block_rows, channels = values.shape
    group_count = bands.shape[0]
    group_width = channels // group_count
    ctx_rank = lax.axis_index("ctx")
    offsets = jnp.arange(block_rows, dtype=jnp.float32)[:, None]
    lengths = jnp.repeat(
        (bands + 1) * block_rows, group_width, total_repeat_length=channels
    ).astype(jnp.float32)
    band_tail = jnp.exp(-decay * lengths)[None, :]
    block_decay = jnp.exp(-decay * block_rows)
    lead_decay = jnp.exp(-decay[None, :] * (offsets + 1.0))
    trail_decay = jnp.exp(-decay[None, :] * (block_rows - offsets))
    zero_state = jnp.zeros_like(decay)
    unit_state = jnp.ones_like(decay)
    inside = local_scan(values, decay, False)
    before, _ = prefix(
        (inside[-1], block_decay), "ctx", chain_step, (zero_state, unit_state), False
    )
    carried = inside + lead_decay * before[None, :]
    send_fwd = slot_groups(bands, ctx_rank, 1)
    source_fwd = ctx_rank - bands - 1
    valid_fwd = source_fwd >= 0
    source_fwd = jnp.clip(source_fwd, 0, group_count - 1)
    inside_back = local_scan(upstream, decay, True)
    after, _ = prefix(
        (inside_back[0], block_decay), "ctx", chain_step, (zero_state, unit_state), True
    )
    back_carried = inside_back + trail_decay * after[None, :]
    send_bwd = slot_groups(bands, ctx_rank, -1)
    source_bwd = ctx_rank + bands + 1
    valid_bwd = source_bwd < group_count
    source_bwd = jnp.clip(source_bwd, 0, group_count - 1)
    received = lax.all_to_all(
        outgoing(carried, send_fwd, group_count, group_width),
        "ctx",
        split_axis=1,
        concat_axis=1,
        tiled=True,
    )
    far_state = incoming(received, source_fwd, valid_fwd)
    received_back = lax.all_to_all(
        outgoing(back_carried, send_bwd, group_count, group_width),
        "ctx",
        split_axis=1,
        concat_axis=1,
        tiled=True,
    )
    near_state = incoming(received_back, source_bwd, valid_bwd)
    truncated = carried - band_tail * far_state
    layer_out = (skip_gain[None, :] * values + residue[None, :] * truncated).astype(jnp.bfloat16)
    back_truncated = back_carried - band_tail * near_state
    input_grad = (skip_gain[None, :] * upstream + residue[None, :] * back_truncated).astype(
        jnp.bfloat16
    )
    position = ctx_rank.astype(jnp.float32) * block_rows + offsets
    weighted = upstream * truncated
    moment = jnp.sum(position * weighted, axis=0) - jnp.sum(
        position * values * back_truncated, axis=0
    )
    grad_terms = jnp.stack(
        [jnp.sum(values * upstream, axis=0), jnp.sum(weighted, axis=0), -decay * residue * moment]
    )
    share_width = channels // lax.axis_size("ctx")
    summed = lax.psum(grad_terms, "ctx")
    own_share = lax.dynamic_slice_in_dim(summed, ctx_rank * share_width, share_width, 1)
    return (layer_out, input_grad, own_share[0], own_share[1], own_share[2])


MESH = pl.DeviceIdType.MESH
LANES = 128
ROWS = 8


def greet(count, me):
    barrier = pltpu.get_barrier_semaphore()
    for step in range(1, count):
        pl.semaphore_signal(
            barrier,
            inc=1,
            device_id={"ctx": lax.rem(me + step, count)},
            device_id_type=MESH,
        )
    pl.semaphore_wait(barrier, count - 1)


def pack_kernel(bands_ref, x_ref, c_ref, decay_ref, xs_ref, cs_ref, ends_ref):
    del bands_ref
    rows, width = x_ref.shape
    xs_ref[0] = x_ref[...]
    cs_ref[0] = c_ref[...]
    rate = decay_ref[...]
    level = lax.broadcasted_iota(jnp.int32, (ROWS, width), 0).astype(jnp.float32)
    leap = jnp.broadcast_to(jnp.exp(-rate * (2 * ROWS)), (ROWS, width))
    steps = rows // (2 * ROWS)

    def turn(step, sums):
        ahead = x_ref[pl.ds(pl.multiple_of(step * 2 * ROWS, 2 * ROWS), 2 * ROWS), :]
        back = c_ref[
            pl.ds(pl.multiple_of((steps - 1 - step) * 2 * ROWS, 2 * ROWS), 2 * ROWS), :
        ]
        ahead = ahead.astype(jnp.float32)
        back = back.astype(jnp.float32)
        return (
            sums[0] * leap + ahead[:ROWS],
            sums[1] * leap + ahead[ROWS:],
            sums[2] * leap + back[:ROWS],
            sums[3] * leap + back[ROWS:],
        )

    zero = jnp.zeros((ROWS, width), jnp.float32)
    upper, lower, back_upper, back_lower = lax.fori_loop(
        0, steps, turn, (zero, zero, zero, zero), unroll=4
    )
    last = upper * jnp.exp(-rate * (2 * ROWS - 1 - level)) + lower * jnp.exp(
        -rate * (ROWS - 1 - level)
    )
    first = back_upper * jnp.exp(-rate * level) + back_lower * jnp.exp(-rate * (ROWS + level))
    ends_ref[0:1, :] = jnp.sum(last, axis=0, keepdims=True)
    ends_ref[1:2, :] = jnp.sum(first, axis=0, keepdims=True)


def pack(bands, inputs, cotangent, decay):
    rows, channels = inputs.shape
    groups = bands.shape[0]
    width = channels // groups
    block = pl.BlockSpec((rows, width), lambda g, bands: (0, g))
    slot = pl.BlockSpec((1, rows, width), lambda g, bands: (bands[g], 0, 0))
    return pl.pallas_call(
        pack_kernel,
        grid_spec=pltpu.PrefetchScalarGridSpec(
            num_scalar_prefetch=1,
            grid=(groups,),
            in_specs=[block, block, pl.BlockSpec((1, width), lambda g, bands: (0, g))],
            out_specs=[slot, slot, pl.BlockSpec((2, width), lambda g, bands: (0, g))],
        ),
        out_shape=(
            jax.ShapeDtypeStruct((groups, rows, width), inputs.dtype),
            jax.ShapeDtypeStruct((groups, rows, width), inputs.dtype),
            jax.ShapeDtypeStruct((2, channels), jnp.float32),
        ),
        name="pack",
    )(bands, inputs, cotangent, decay)


def swap_kernel(
    count, xs, cs, ends, far_x, far_c, far_ends, x_send, x_recv, c_send, c_recv, e_send, e_recv
):
    me = lax.axis_index("ctx")
    greet(count, me)

    def end_copy(step):
        return pltpu.make_async_remote_copy(
            src_ref=ends,
            dst_ref=far_ends.at[me],
            send_sem=e_send.at[step],
            recv_sem=e_recv.at[step],
            device_id={"ctx": lax.rem(me + step + 1, count)},
            device_id_type=MESH,
        )

    def x_copy(slot):
        return pltpu.make_async_remote_copy(
            src_ref=xs.at[slot],
            dst_ref=far_x.at[slot],
            send_sem=x_send.at[slot],
            recv_sem=x_recv.at[slot],
            device_id={"ctx": lax.rem(me + slot + 1, count)},
            device_id_type=MESH,
        )

    def c_copy(slot):
        return pltpu.make_async_remote_copy(
            src_ref=cs.at[slot],
            dst_ref=far_c.at[slot],
            send_sem=c_send.at[slot],
            recv_sem=c_recv.at[slot],
            device_id={"ctx": lax.rem(me + count - slot - 1, count)},
            device_id_type=MESH,
        )

    for step in range(count - 1):
        end_copy(step).start()
    for slot in range(count - 1):
        hop = slot + 1
        pl.when(me + hop < count)(lambda: x_copy(slot).start())
        pl.when(me >= hop)(lambda: c_copy(slot).start())
    for step in range(count - 1):
        end_copy(step).wait()
    for slot in range(count - 1):
        hop = slot + 1

        @pl.when(me + hop < count)
        def _():
            x_copy(slot).wait_send()
            c_copy(slot).wait_recv()

        @pl.when(me >= hop)
        def _():
            c_copy(slot).wait_send()
            x_copy(slot).wait_recv()


def swap(count, xs, cs, ends):
    groups, rows, width = xs.shape
    far = jax.ShapeDtypeStruct((count - 1, rows, width), xs.dtype)
    anywhere = pl.BlockSpec(memory_space=pl.ANY)
    one = pltpu.SemaphoreType.DMA((count - 1,))
    return pl.pallas_call(
        functools.partial(swap_kernel, count),
        in_specs=[anywhere] * 3,
        out_specs=[anywhere] * 3,
        out_shape=(far, far, jax.ShapeDtypeStruct((count,) + ends.shape, ends.dtype)),
        scratch_shapes=[one] * 6,
        compiler_params=pltpu.CompilerParams(collective_id=0, has_side_effects=True),
        name="swap",
    )(xs, cs, ends)


def finish_kernel(
    count,
    tiles_wide,
    bands_ref,
    x_ref,
    c_ref,
    far_x_ref,
    far_c_ref,
    ends_ref,
    residue_ref,
    decay_ref,
    skip_ref,
    out_ref,
    grad_ref,
    sums_ref,
):
    me = lax.axis_index("ctx")
    band = bands_ref[pl.program_id(0)] + 1
    rows, width = x_ref.shape
    has_before = me >= band
    has_after = me + band < count
    rate = decay_ref[...]
    shape = (ROWS, width)
    carry = jnp.zeros((1, width), jnp.float32)
    back_carry = carry
    for other in range(count):
        apart = me - 1 - other
        kept = jnp.logical_and(apart >= 0, apart < band)
        factor = jnp.exp(-rate * (jnp.maximum(apart, 0) * rows).astype(jnp.float32))
        carry = carry + jnp.where(kept, factor * ends_ref[other, 0:1, :], 0.0)
        apart = other - me - 1
        kept = jnp.logical_and(apart >= 0, apart < band)
        factor = jnp.exp(-rate * (jnp.maximum(apart, 0) * rows).astype(jnp.float32))
        back_carry = back_carry + jnp.where(kept, factor * ends_ref[other, 1:2, :], 0.0)
    tail = jnp.broadcast_to(jnp.exp(-rate * (band * rows).astype(jnp.float32)), shape)
    level = lax.broadcasted_iota(jnp.int32, shape, 0)
    depth = level.astype(jnp.float32)
    fwd = [
        (hop, jnp.where(level >= hop, jnp.exp(-rate * hop), 0.0)) for hop in (1, 2, 4)
    ]
    bwd = [
        (ROWS - hop, jnp.where(level < ROWS - hop, jnp.exp(-rate * hop), 0.0))
        for hop in (1, 2, 4)
    ]
    lead = jnp.exp(-rate * (depth + 1.0))
    trail = jnp.exp(-rate * (ROWS - depth))
    leap = jnp.broadcast_to(jnp.exp(-rate * ROWS), shape)
    residue = jnp.broadcast_to(residue_ref[...], shape)
    skip = jnp.broadcast_to(skip_ref[...], shape)
    steps = rows // (2 * ROWS)

    def scan(tile, hops):
        for hop, factor in hops:
            tile = tile + factor * pltpu.roll(tile, hop, 0)
        return tile

    def turn(step, state):
        carry, back_carry, s_skip, s_w, s_tw, s_v, s_tv = state
        at = pl.ds(pl.multiple_of(step * 2 * ROWS, 2 * ROWS), 2 * ROWS)
        base = (step * (2 * ROWS)).astype(jnp.float32)
        x = x_ref[at, :].astype(jnp.float32)
        c = c_ref[at, :].astype(jnp.float32)
        far = far_x_ref[0, at, :].astype(jnp.float32)
        outs = []
        for half in range(2):
            part = slice(half * ROWS, (half + 1) * ROWS)
            local = scan(
                x[part] - jnp.where(has_before, tail * far[part], 0.0), fwd
            )
            truncated = local + lead * carry
            carry = leap * carry + jnp.broadcast_to(local[ROWS - 1 :], shape)
            outs.append(skip * x[part] + residue * truncated)
            w = c[part] * truncated
            s_skip = s_skip + x[part] * c[part]
            s_w = s_w + w
            s_tw = s_tw + (base + half * ROWS) * w
        out_ref[at, :] = jnp.concatenate(outs, axis=0).astype(out_ref.dtype)
        at = pl.ds(pl.multiple_of((steps - 1 - step) * 2 * ROWS, 2 * ROWS), 2 * ROWS)
        base = ((steps - 1 - step) * (2 * ROWS)).astype(jnp.float32)
        x = x_ref[at, :].astype(jnp.float32)
        c = c_ref[at, :].astype(jnp.float32)
        far = far_c_ref[0, at, :].astype(jnp.float32)
        outs = [None, None]
        for half in (1, 0):
            part = slice(half * ROWS, (half + 1) * ROWS)
            local = scan(c[part] - jnp.where(has_after, tail * far[part], 0.0), bwd)
            truncated = local + trail * back_carry
            back_carry = leap * back_carry + jnp.broadcast_to(local[:1], shape)
            outs[half] = skip * c[part] + residue * truncated
            v = x[part] * truncated
            s_v = s_v + v
            s_tv = s_tv + (base + half * ROWS) * v
        grad_ref[at, :] = jnp.concatenate(outs, axis=0).astype(grad_ref.dtype)
        return carry, back_carry, s_skip, s_w, s_tw, s_v, s_tv

    zero = jnp.zeros(shape, jnp.float32)
    state = (
        jnp.broadcast_to(carry, shape),
        jnp.broadcast_to(back_carry, shape),
        zero,
        zero,
        zero,
        zero,
        zero,
    )
    _, _, s_skip, s_w, s_tw, s_v, s_tv = lax.fori_loop(0, steps, turn, state, unroll=4)
    offset = depth + (me * rows).astype(jnp.float32)
    moment = (s_tw - s_tv) + offset * (s_w - s_v)
    sums_ref[0, 0:1, :] = jnp.sum(s_skip, axis=0, keepdims=True)
    sums_ref[0, 1:2, :] = jnp.sum(s_w, axis=0, keepdims=True)
    sums_ref[0, 2:3, :] = (
        -rate * residue_ref[...] * jnp.sum(moment, axis=0, keepdims=True)
    )


def finish(count, bands, x, c, far_x, far_c, ends, residue, decay, skip):
    rows, channels = x.shape
    groups = bands.shape[0]
    wide = channels // groups // LANES
    block = pl.BlockSpec((rows, LANES), lambda g, l, bands: (0, g * wide + l))
    far = pl.BlockSpec(
        (1, rows, LANES), lambda g, l, bands: (jnp.minimum(bands[g], groups - 2), 0, l)
    )
    row = pl.BlockSpec((1, LANES), lambda g, l, bands: (0, g * wide + l))
    return pl.pallas_call(
        functools.partial(finish_kernel, count, wide),
        grid_spec=pltpu.PrefetchScalarGridSpec(
            num_scalar_prefetch=1,
            grid=(groups, wide),
            in_specs=[
                block,
                block,
                far,
                far,
                pl.BlockSpec((count, 2, LANES), lambda g, l, bands: (0, 0, g * wide + l)),
                row,
                row,
                row,
            ],
            out_specs=[
                block,
                block,
                pl.BlockSpec((1, ROWS, LANES), lambda g, l, bands: (g, 0, l)),
            ],
        ),
        out_shape=(
            jax.ShapeDtypeStruct((rows, channels), x.dtype),
            jax.ShapeDtypeStruct((rows, channels), x.dtype),
            jax.ShapeDtypeStruct((groups, ROWS, channels // groups), jnp.float32),
        ),
        name="finish",
    )(bands, x, c, far_x, far_c, ends, residue, decay, skip)


def total_kernel(count, sums, total_ref, got, send, recv):
    me = lax.axis_index("ctx")
    greet(count, me)

    def copy(step):
        peer = lax.rem(me + step + 1, count)
        return pltpu.make_async_remote_copy(
            src_ref=sums.at[peer],
            dst_ref=got.at[step],
            send_sem=send.at[step],
            recv_sem=recv.at[step],
            device_id={"ctx": peer},
            device_id_type=MESH,
        )

    for step in range(count - 1):
        copy(step).start()
    total = sums[me]
    for step in range(count - 1):
        copy(step).wait()
        total = total + got[step]
    total_ref[...] = total


def total(count, sums):
    inside = pl.BlockSpec(memory_space=pltpu.VMEM)
    one = pltpu.SemaphoreType.DMA((count - 1,))
    return pl.pallas_call(
        functools.partial(total_kernel, count),
        in_specs=[inside],
        out_specs=inside,
        out_shape=jax.ShapeDtypeStruct(sums.shape[1:], sums.dtype),
        scratch_shapes=[
            pltpu.VMEM((count - 1,) + sums.shape[1:], sums.dtype),
            one,
            one,
        ],
        compiler_params=pltpu.CompilerParams(collective_id=1, has_side_effects=True),
        name="total",
    )(sums)


def banded(count, inputs, cotangent, residue, decay, skip_gain, band_blocks):
    bands = band_blocks[0]
    residue, decay, skip_gain = (part[None, :] for part in (residue, decay, skip_gain))
    xs, cs, ends = pack(bands, inputs, cotangent, decay)
    far_x, far_c, far_ends = swap(count, xs, cs, ends)
    layer_out, input_grad, sums = finish(
        count, bands, inputs, cotangent, far_x, far_c, far_ends, residue, decay, skip_gain
    )
    own = total(count, sums)
    return (layer_out, input_grad, own[0], own[1], own[2])


def local_body(count, inputs, cotangent, residue, decay, skip_gain, band_blocks):
    rows, channels = inputs.shape
    groups = band_blocks.shape[1]
    fits = groups == count and count > 1 and rows % (2 * ROWS) == 0
    if fits and channels % (groups * LANES) == 0:
        return banded(count, inputs, cotangent, residue, decay, skip_gain, band_blocks)
    return body(inputs, cotangent, residue, decay, skip_gain, band_blocks)


def solution(mesh):
    placed = (P("ctx", "dp"), P("ctx", "dp"), P("dp"), P("dp"), P("dp"), P("dp", None))
    return jax.shard_map(
        functools.partial(local_body, mesh.shape["ctx"]),
        mesh=mesh,
        in_specs=placed,
        out_specs=(
            P("ctx", "dp"),
            P("ctx", "dp"),
            P(("dp", "ctx")),
            P(("dp", "ctx")),
            P(("dp", "ctx")),
        ),
        check_vma=False,
    )
```

```python
import functools
import jax
import jax.numpy as jnp
from jax import lax
from jax.experimental import pallas as pl
from jax.experimental.pallas import tpu as pltpu
from jax.sharding import PartitionSpec as P


def prefix(value, axis, join, neutral, backward):
    count, mine = (lax.axis_size(axis), lax.axis_index(axis))
    pieces = jax.tree.map(lambda part: lax.all_gather(part, axis), value)
    if backward:
        pieces = jax.tree.map(lambda part: part[::-1], pieces)
        mine = count - 1 - mine
    total = jax.tree.map(
        lambda part, zero: jnp.full_like(part, 0) + jnp.asarray(zero, part.dtype), value, neutral
    )

    def turn(position, total):
        longer = join(total, jax.tree.map(lambda part: part[position], pieces))
        return jax.tree.map(lambda new, old: jnp.where(position < mine, new, old), longer, total)

    return lax.fori_loop(0, count - 1, turn, total)


def compose(earlier_pair, later_pair):
    return (earlier_pair[0] * later_pair[0], earlier_pair[1] * later_pair[0] + later_pair[1])


def chain_step(earlier_pair, later_pair):
    return (earlier_pair[0] * later_pair[1] + later_pair[0], earlier_pair[1] * later_pair[1])


def local_scan(values, decay_rate, backward):
    factors = jnp.broadcast_to(jnp.exp(-decay_rate)[None, :], values.shape)
    return lax.associative_scan(compose, (factors, values), reverse=backward)[1]


def slot_groups(bands, ctx_rank, direction):
    group_count = bands.shape[0]
    slot_index = jnp.arange(group_count, dtype=jnp.int32)
    distance = (slot_index - ctx_rank) * direction
    matches = bands[None, :] + 1 == distance[:, None]
    return jnp.sum(jnp.where(matches, slot_index[None, :], 0), axis=1)


def outgoing(values, slot_group, group_count, group_width):
    shaped = values.reshape(values.shape[0], group_count, group_width)
    return jnp.take(shaped, slot_group, axis=1)


def incoming(received, source, in_range):
    picked = jnp.take(received, source, axis=1)
    picked = jnp.where(in_range[None, :, None], picked, jnp.zeros((), picked.dtype))
    return picked.reshape(picked.shape[0], -1)


def body(inputs, cotangent, residue, decay, skip_gain, band_blocks):
    values = inputs.astype(jnp.float32)
    upstream = cotangent.astype(jnp.float32)
    bands = band_blocks[0]
    block_rows, channels = values.shape
    group_count = bands.shape[0]
    group_width = channels // group_count
    ctx_rank = lax.axis_index("ctx")
    offsets = jnp.arange(block_rows, dtype=jnp.float32)[:, None]
    lengths = jnp.repeat(
        (bands + 1) * block_rows, group_width, total_repeat_length=channels
    ).astype(jnp.float32)
    band_tail = jnp.exp(-decay * lengths)[None, :]
    block_decay = jnp.exp(-decay * block_rows)
    lead_decay = jnp.exp(-decay[None, :] * (offsets + 1.0))
    trail_decay = jnp.exp(-decay[None, :] * (block_rows - offsets))
    zero_state = jnp.zeros_like(decay)
    unit_state = jnp.ones_like(decay)
    inside = local_scan(values, decay, False)
    before, _ = prefix(
        (inside[-1], block_decay), "ctx", chain_step, (zero_state, unit_state), False
    )
    carried = inside + lead_decay * before[None, :]
    send_fwd = slot_groups(bands, ctx_rank, 1)
    source_fwd = ctx_rank - bands - 1
    valid_fwd = source_fwd >= 0
    source_fwd = jnp.clip(source_fwd, 0, group_count - 1)
    inside_back = local_scan(upstream, decay, True)
    after, _ = prefix(
        (inside_back[0], block_decay), "ctx", chain_step, (zero_state, unit_state), True
    )
    back_carried = inside_back + trail_decay * after[None, :]
    send_bwd = slot_groups(bands, ctx_rank, -1)
    source_bwd = ctx_rank + bands + 1
    valid_bwd = source_bwd < group_count
    source_bwd = jnp.clip(source_bwd, 0, group_count - 1)
    received = lax.all_to_all(
        outgoing(carried, send_fwd, group_count, group_width),
        "ctx",
        split_axis=1,
        concat_axis=1,
        tiled=True,
    )
    far_state = incoming(received, source_fwd, valid_fwd)
    received_back = lax.all_to_all(
        outgoing(back_carried, send_bwd, group_count, group_width),
        "ctx",
        split_axis=1,
        concat_axis=1,
        tiled=True,
    )
    near_state = incoming(received_back, source_bwd, valid_bwd)
    truncated = carried - band_tail * far_state
    layer_out = (skip_gain[None, :] * values + residue[None, :] * truncated).astype(jnp.bfloat16)
    back_truncated = back_carried - band_tail * near_state
    input_grad = (skip_gain[None, :] * upstream + residue[None, :] * back_truncated).astype(
        jnp.bfloat16
    )
    position = ctx_rank.astype(jnp.float32) * block_rows + offsets
    weighted = upstream * truncated
    moment = jnp.sum(position * weighted, axis=0) - jnp.sum(
        position * values * back_truncated, axis=0
    )
    grad_terms = jnp.stack(
        [jnp.sum(values * upstream, axis=0), jnp.sum(weighted, axis=0), -decay * residue * moment]
    )
    share_width = channels // lax.axis_size("ctx")
    summed = lax.psum(grad_terms, "ctx")
    own_share = lax.dynamic_slice_in_dim(summed, ctx_rank * share_width, share_width, 1)
    return (layer_out, input_grad, own_share[0], own_share[1], own_share[2])


MESH = pl.DeviceIdType.MESH
LANES = 128
ROWS = 8
PAIR = 2 * ROWS
PIECES = 4
UNROLL = 4


def greet(count, me):
    barrier = pltpu.get_barrier_semaphore()
    for step in range(1, count):
        pl.semaphore_signal(
            barrier,
            inc=1,
            device_id={"ctx": lax.rem(me + step, count)},
            device_id_type=MESH,
        )
    return lambda: pl.semaphore_wait(barrier, count - 1)


def pieces_of(count, slot):
    return PIECES if slot == count - 2 else 1


def pair_at(step):
    return pl.ds(pl.multiple_of(step * PAIR, PAIR), PAIR)


def banded_kernel(
    count,
    bands,
    x_hbm,
    c_hbm,
    residue_ref,
    decay_ref,
    skip_ref,
    out_hbm,
    grad_hbm,
    total_ref,
    x_all,
    c_all,
    xs,
    cs,
    far_x,
    far_c,
    ends,
    far_ends,
    outs,
    grads,
    sums,
    got,
    load_sem,
    store_sem,
    x_send,
    x_recv,
    c_send,
    c_recv,
    e_send,
    e_recv,
    s_send,
    s_recv,
):
    me = lax.axis_index("ctx")
    _, rows, width = x_all.shape
    shape = (ROWS, width)
    steps = rows // PAIR

    def load(source, target, at, group):
        lanes = pl.ds(group * width, width)
        return pltpu.make_async_copy(
            source.at[:, lanes], target.at[group], load_sem.at[at, group]
        )

    for at, (source, target) in enumerate(((x_hbm, x_all), (c_hbm, c_all))):
        for group in range(count):
            load(source, target, at, group).start()
    all_here = greet(count, me)
    groups = []
    for slot in range(count):
        group = jnp.int32(0)
        for other in range(count):
            group = jnp.where(bands[other] == slot, other, group)
        groups.append(group)

    def pack(whole, packed):
        def turn(step, _):
            at = pair_at(step)
            for slot in range(count):
                packed[slot, at, :] = whole[groups[slot], at, :]
            return 0

        lax.fori_loop(0, steps, turn, 0, unroll=UNROLL)

    for at, (source, target, packed) in enumerate(((x_hbm, x_all, xs), (c_hbm, c_all, cs))):
        for group in range(count):
            load(source, target, at, group).wait()
        pack(target, packed)

    first_sem = [sum(pieces_of(count, s) for s in range(slot)) for slot in range(count)]

    def x_copy(slot, piece):
        size = rows // pieces_of(count, slot)
        at = pl.ds(piece * size, size)
        sem = first_sem[slot] + piece
        return pltpu.make_async_remote_copy(
            src_ref=xs.at[slot, at],
            dst_ref=far_x.at[slot, at],
            send_sem=x_send.at[sem],
            recv_sem=x_recv.at[sem],
            device_id={"ctx": lax.rem(me + slot + 1, count)},
            device_id_type=MESH,
        )

    def c_copy(slot, piece):
        size = rows // pieces_of(count, slot)
        at = pl.ds(rows - (piece + 1) * size, size)
        sem = first_sem[slot] + piece
        return pltpu.make_async_remote_copy(
            src_ref=cs.at[slot, at],
            dst_ref=far_c.at[slot, at],
            send_sem=c_send.at[sem],
            recv_sem=c_recv.at[sem],
            device_id={"ctx": lax.rem(me + count - slot - 1, count)},
            device_id_type=MESH,
        )

    def small_copy(source, target, send, recv, step):
        return pltpu.make_async_remote_copy(
            src_ref=source,
            dst_ref=target,
            send_sem=send.at[step],
            recv_sem=recv.at[step],
            device_id={"ctx": lax.rem(me + step + 1, count)},
            device_id_type=MESH,
        )

    def end_copy(step):
        return small_copy(ends, far_ends.at[me], e_send, e_recv, step)

    def share_copy(slot, step):
        at = slot * (count - 1) + step
        return pltpu.make_async_remote_copy(
            src_ref=sums.at[slot],
            dst_ref=got.at[step, slot],
            send_sem=s_send.at[at],
            recv_sem=s_recv.at[at],
            device_id={"ctx": lax.rem(me + step + 1, count)},
            device_id_type=MESH,
        )

    def store(slot, piece, backward):
        pieces = pieces_of(count, slot)
        size = rows // pieces
        source, target = (grads, grad_hbm) if backward else (outs, out_hbm)
        at = pl.ds(rows - (piece + 1) * size if backward else piece * size, size)
        sem = store_sem.at[int(backward), first_sem[slot] + piece]
        return pltpu.make_async_copy(source.at[slot, at], target.at[slot, at], sem)

    def send(slot):
        for piece in range(pieces_of(count, slot)):
            pl.when(me + slot + 1 < count)(lambda: x_copy(slot, piece).start())
            pl.when(me >= slot + 1)(lambda: c_copy(slot, piece).start())

    all_here()
    send(0)

    level = lax.broadcasted_iota(jnp.int32, shape, 0)
    depth = level.astype(jnp.float32)
    zero = jnp.zeros(shape, jnp.float32)
    for slot in range(count):
        rate = decay_ref[groups[slot]]
        leap_pair = jnp.broadcast_to(jnp.exp(-rate * PAIR), shape)

        def turn(step, held):
            ahead = xs[slot, pair_at(step), :].astype(jnp.float32)
            back = cs[slot, pair_at(steps - 1 - step), :].astype(jnp.float32)
            parts = (ahead[:ROWS], ahead[ROWS:], back[:ROWS], back[ROWS:])
            return tuple(old * leap_pair + new for old, new in zip(held, parts))

        upper, lower, back_upper, back_lower = lax.fori_loop(
            0, steps, turn, (zero,) * 4, unroll=UNROLL
        )
        last = upper * jnp.exp(-rate * (PAIR - 1 - depth)) + lower * jnp.exp(
            -rate * (ROWS - 1 - depth)
        )
        first = back_upper * jnp.exp(-rate * depth) + back_lower * jnp.exp(
            -rate * (ROWS + depth)
        )
        ends[slot, 0:1, :] = jnp.sum(last, axis=0, keepdims=True)
        ends[slot, 1:2, :] = jnp.sum(first, axis=0, keepdims=True)
    for step in range(count - 1):
        end_copy(step).start()
    for slot in range(1, count - 1):
        send(slot)
    for step in range(count - 1):
        end_copy(step).wait()

    def scan(tile, hops):
        for hop, factor in hops:
            tile = tile + factor * pltpu.roll(tile, hop, 0)
        return tile

    def work(slot):
        band = slot + 1
        has_before = me >= band
        has_after = me + band < count
        reach = slot < count - 1
        rate = decay_ref[groups[slot]]
        residue_row = residue_ref[groups[slot]]
        carry = jnp.zeros((1, width), jnp.float32)
        back_carry = carry
        for other in range(count):
            apart = me - 1 - other
            kept = jnp.logical_and(apart >= 0, apart < band)
            factor = jnp.exp(-rate * (jnp.maximum(apart, 0) * rows).astype(jnp.float32))
            carry = carry + jnp.where(kept, factor * far_ends[other, slot, 0:1, :], 0.0)
            apart = other - me - 1
            kept = jnp.logical_and(apart >= 0, apart < band)
            factor = jnp.exp(-rate * (jnp.maximum(apart, 0) * rows).astype(jnp.float32))
            back_carry = back_carry + jnp.where(
                kept, factor * far_ends[other, slot, 1:2, :], 0.0
            )
        tail = jnp.broadcast_to(jnp.exp(-rate * float(band * rows)), shape)
        leap = jnp.broadcast_to(jnp.exp(-rate * ROWS), shape)
        residue = jnp.broadcast_to(residue_row, shape)
        skip = jnp.broadcast_to(skip_ref[groups[slot]], shape)
        lead = jnp.exp(-rate * (depth + 1.0))
        trail = jnp.exp(-rate * (ROWS - depth))
        fwd = [
            (hop, jnp.where(level >= hop, jnp.exp(-rate * hop), 0.0)) for hop in (1, 2, 4)
        ]
        bwd = [
            (ROWS - hop, jnp.where(level < ROWS - hop, jnp.exp(-rate * hop), 0.0))
            for hop in (1, 2, 4)
        ]

        def forward(step, state):
            carry, s_skip, s_w, s_tw = state
            at = pair_at(step)
            base = (step * PAIR).astype(jnp.float32)
            x = xs[slot, at, :].astype(jnp.float32)
            c = cs[slot, at, :].astype(jnp.float32)
            if reach:
                far = far_x[slot, at, :].astype(jnp.float32)
            made = []
            for half in range(2):
                part = slice(half * ROWS, (half + 1) * ROWS)
                fresh = x[part]
                if reach:
                    fresh = fresh - jnp.where(has_before, tail * far[part], 0.0)
                local = scan(fresh, fwd)
                truncated = local + lead * carry
                carry = leap * carry + jnp.broadcast_to(local[ROWS - 1 :], shape)
                made.append(skip * x[part] + residue * truncated)
                w = c[part] * truncated
                s_skip = s_skip + x[part] * c[part]
                s_w = s_w + w
                s_tw = s_tw + (base + half * ROWS) * w
            outs[slot, at, :] = jnp.concatenate(made, axis=0).astype(outs.dtype)
            return carry, s_skip, s_w, s_tw

        def backward(step, state):
            carry, s_v, s_tv = state
            at = pair_at(steps - 1 - step)
            base = ((steps - 1 - step) * PAIR).astype(jnp.float32)
            x = xs[slot, at, :].astype(jnp.float32)
            c = cs[slot, at, :].astype(jnp.float32)
            if reach:
                far = far_c[slot, at, :].astype(jnp.float32)
            made = [None, None]
            for half in (1, 0):
                part = slice(half * ROWS, (half + 1) * ROWS)
                fresh = c[part]
                if reach:
                    fresh = fresh - jnp.where(has_after, tail * far[part], 0.0)
                local = scan(fresh, bwd)
                truncated = local + trail * carry
                carry = leap * carry + jnp.broadcast_to(local[:1], shape)
                made[half] = skip * c[part] + residue * truncated
                v = x[part] * truncated
                s_v = s_v + v
                s_tv = s_tv + (base + half * ROWS) * v
            grads[slot, at, :] = jnp.concatenate(made, axis=0).astype(grads.dtype)
            return carry, s_v, s_tv

        ahead = (jnp.broadcast_to(carry, shape), zero, zero, zero)
        back = (jnp.broadcast_to(back_carry, shape), zero, zero)
        pieces = pieces_of(count, slot)
        for piece in range(pieces):
            span = (piece * steps // pieces, (piece + 1) * steps // pieces)
            if reach:
                pl.when(has_before)(lambda: x_copy(slot, piece).wait_recv())
            ahead = lax.fori_loop(*span, forward, ahead, unroll=UNROLL)
            store(slot, piece, False).start()
            if reach:
                pl.when(has_after)(lambda: c_copy(slot, piece).wait_recv())
            back = lax.fori_loop(*span, backward, back, unroll=UNROLL)
            store(slot, piece, True).start()
        _, s_skip, s_w, s_tw = ahead
        _, s_v, s_tv = back
        offset = depth + (me * rows).astype(jnp.float32)
        moment = (s_tw - s_tv) + offset * (s_w - s_v)
        sums[slot, 0:1, :] = jnp.sum(s_skip, axis=0, keepdims=True)
        sums[slot, 1:2, :] = jnp.sum(s_w, axis=0, keepdims=True)
        sums[slot, 2:3, :] = (
            -rate * residue_row * jnp.sum(moment, axis=0, keepdims=True)
        )
        for step in range(count - 1):
            share_copy(slot, step).start()

    sums[...] = jnp.zeros_like(sums)
    work(count - 1)
    for slot in range(count - 1):
        work(slot)

    for slot in range(count):
        for piece in range(pieces_of(count, slot)):
            store(slot, piece, False).wait()
            store(slot, piece, True).wait()
    for slot in range(count):
        total = sums[slot]
        for step in range(count - 1):
            share_copy(slot, step).wait()
            total = total + got[step, slot]
        total_ref[slot] = total
    for slot in range(count - 1):
        for piece in range(pieces_of(count, slot)):
            pl.when(me + slot + 1 < count)(lambda: x_copy(slot, piece).wait_send())
            pl.when(me >= slot + 1)(lambda: c_copy(slot, piece).wait_send())


def place_kernel(bands, out, grad, total, out_ref, grad_ref, skip_ref, residue_ref, decay_ref):
    out_ref[...] = out[0]
    grad_ref[...] = grad[0]
    own = total[bands[lax.axis_index("ctx")]]
    skip_ref[...] = own[0:1]
    residue_ref[...] = own[1:2]
    decay_ref[...] = own[2:3]


def place(bands, outs, grads, totals):
    count, rows, width = outs.shape
    slot = pl.BlockSpec((1, rows // 2, width), lambda g, r, bands: (bands[g], r, 0))
    block = pl.BlockSpec((rows // 2, width), lambda g, r, bands: (r, g))
    one = pl.BlockSpec((1, width), lambda g, r, bands: (0, 0))
    whole = jax.ShapeDtypeStruct((rows, count * width), outs.dtype)
    small = jax.ShapeDtypeStruct((1, width), totals.dtype)
    return pl.pallas_call(
        place_kernel,
        grid_spec=pltpu.PrefetchScalarGridSpec(
            num_scalar_prefetch=1,
            grid=(count, 2),
            in_specs=[
                slot,
                slot,
                pl.BlockSpec(totals.shape, lambda g, r, bands: (0, 0, 0)),
            ],
            out_specs=[block, block, one, one, one],
        ),
        out_shape=(whole, whole, small, small, small),
        name="place",
    )(bands, outs, grads, totals)


def banded(count, inputs, cotangent, residue, decay, skip_gain, band_blocks):
    rows, channels = inputs.shape
    width = channels // count
    bands = band_blocks[0]
    anywhere = pl.BlockSpec(memory_space=pl.ANY)
    inside = pl.BlockSpec(memory_space=pltpu.VMEM)
    flows = sum(pieces_of(count, slot) for slot in range(count))
    many = pltpu.SemaphoreType.DMA((flows,))
    few = pltpu.SemaphoreType.DMA((count - 1,))
    some = pltpu.SemaphoreType.DMA((count * (count - 1),))
    packed = pltpu.VMEM((count, rows, width), inputs.dtype)
    far = pltpu.VMEM((count - 1, rows, width), inputs.dtype)
    outs, grads, totals = pl.pallas_call(
        functools.partial(banded_kernel, count),
        in_specs=[
            pl.BlockSpec(memory_space=pltpu.SMEM),
            anywhere,
            anywhere,
            inside,
            inside,
            inside,
        ],
        out_specs=[anywhere, anywhere, inside],
        out_shape=(
            jax.ShapeDtypeStruct((count, rows, width), inputs.dtype),
            jax.ShapeDtypeStruct((count, rows, width), inputs.dtype),
            jax.ShapeDtypeStruct((count, ROWS // 2, width), jnp.float32),
        ),
        scratch_shapes=[
            packed,
            packed,
            packed,
            packed,
            far,
            far,
            pltpu.VMEM((count, 2, width), jnp.float32),
            pltpu.VMEM((count, count, 2, width), jnp.float32),
            packed,
            packed,
            pltpu.VMEM((count, ROWS // 2, width), jnp.float32),
            pltpu.VMEM((count - 1, count, ROWS // 2, width), jnp.float32),
            pltpu.SemaphoreType.DMA((2, count)),
            pltpu.SemaphoreType.DMA((2, flows)),
            many,
            many,
            many,
            many,
            few,
            few,
            some,
            some,
        ],
        compiler_params=pltpu.CompilerParams(collective_id=0, has_side_effects=True),
        name="banded",
    )(
        bands,
        inputs,
        cotangent,
        *(part.reshape(count, 1, width) for part in (residue, decay, skip_gain)),
    )
    layer_out, input_grad, *sums = place(bands, outs, grads, totals)
    return (layer_out, input_grad, *(part.reshape(width) for part in sums))


def local_body(count, inputs, cotangent, residue, decay, skip_gain, band_blocks):
    rows, channels = inputs.shape
    groups = band_blocks.shape[1]
    fits = groups == count and count > 1 and rows % (PAIR * PIECES) == 0
    if fits and channels % (groups * LANES) == 0:
        return banded(count, inputs, cotangent, residue, decay, skip_gain, band_blocks)
    return body(inputs, cotangent, residue, decay, skip_gain, band_blocks)


def solution(mesh):
    placed = (P("ctx", "dp"), P("ctx", "dp"), P("dp"), P("dp"), P("dp"), P("dp", None))
    return jax.shard_map(
        functools.partial(local_body, mesh.shape["ctx"]),
        mesh=mesh,
        in_specs=placed,
        out_specs=(
            P("ctx", "dp"),
            P("ctx", "dp"),
            P(("dp", "ctx")),
            P(("dp", "ctx")),
            P(("dp", "ctx")),
        ),
        check_vma=False,
    )
```

```python
import functools
import jax
import jax.numpy as jnp
from jax import lax
from jax.experimental import pallas as pl
from jax.experimental.pallas import tpu as pltpu
from jax.sharding import PartitionSpec as P


def prefix(value, axis, join, neutral, backward):
    count, mine = (lax.axis_size(axis), lax.axis_index(axis))
    pieces = jax.tree.map(lambda part: lax.all_gather(part, axis), value)
    if backward:
        pieces = jax.tree.map(lambda part: part[::-1], pieces)
        mine = count - 1 - mine
    total = jax.tree.map(
        lambda part, zero: jnp.full_like(part, 0) + jnp.asarray(zero, part.dtype), value, neutral
    )

    def turn(position, total):
        longer = join(total, jax.tree.map(lambda part: part[position], pieces))
        return jax.tree.map(lambda new, old: jnp.where(position < mine, new, old), longer, total)

    return lax.fori_loop(0, count - 1, turn, total)


def compose(earlier_pair, later_pair):
    return (earlier_pair[0] * later_pair[0], earlier_pair[1] * later_pair[0] + later_pair[1])


def chain_step(earlier_pair, later_pair):
    return (earlier_pair[0] * later_pair[1] + later_pair[0], earlier_pair[1] * later_pair[1])


def local_scan(values, decay_rate, backward):
    factors = jnp.broadcast_to(jnp.exp(-decay_rate)[None, :], values.shape)
    return lax.associative_scan(compose, (factors, values), reverse=backward)[1]


def slot_groups(bands, ctx_rank, direction):
    group_count = bands.shape[0]
    slot_index = jnp.arange(group_count, dtype=jnp.int32)
    distance = (slot_index - ctx_rank) * direction
    matches = bands[None, :] + 1 == distance[:, None]
    return jnp.sum(jnp.where(matches, slot_index[None, :], 0), axis=1)


def outgoing(values, slot_group, group_count, group_width):
    shaped = values.reshape(values.shape[0], group_count, group_width)
    return jnp.take(shaped, slot_group, axis=1)


def incoming(received, source, in_range):
    picked = jnp.take(received, source, axis=1)
    picked = jnp.where(in_range[None, :, None], picked, jnp.zeros((), picked.dtype))
    return picked.reshape(picked.shape[0], -1)


def body(inputs, cotangent, residue, decay, skip_gain, band_blocks):
    values = inputs.astype(jnp.float32)
    upstream = cotangent.astype(jnp.float32)
    bands = band_blocks[0]
    block_rows, channels = values.shape
    group_count = bands.shape[0]
    group_width = channels // group_count
    ctx_rank = lax.axis_index("ctx")
    offsets = jnp.arange(block_rows, dtype=jnp.float32)[:, None]
    lengths = jnp.repeat(
        (bands + 1) * block_rows, group_width, total_repeat_length=channels
    ).astype(jnp.float32)
    band_tail = jnp.exp(-decay * lengths)[None, :]
    block_decay = jnp.exp(-decay * block_rows)
    lead_decay = jnp.exp(-decay[None, :] * (offsets + 1.0))
    trail_decay = jnp.exp(-decay[None, :] * (block_rows - offsets))
    zero_state = jnp.zeros_like(decay)
    unit_state = jnp.ones_like(decay)
    inside = local_scan(values, decay, False)
    before, _ = prefix(
        (inside[-1], block_decay), "ctx", chain_step, (zero_state, unit_state), False
    )
    carried = inside + lead_decay * before[None, :]
    send_fwd = slot_groups(bands, ctx_rank, 1)
    source_fwd = ctx_rank - bands - 1
    valid_fwd = source_fwd >= 0
    source_fwd = jnp.clip(source_fwd, 0, group_count - 1)
    inside_back = local_scan(upstream, decay, True)
    after, _ = prefix(
        (inside_back[0], block_decay), "ctx", chain_step, (zero_state, unit_state), True
    )
    back_carried = inside_back + trail_decay * after[None, :]
    send_bwd = slot_groups(bands, ctx_rank, -1)
    source_bwd = ctx_rank + bands + 1
    valid_bwd = source_bwd < group_count
    source_bwd = jnp.clip(source_bwd, 0, group_count - 1)
    received = lax.all_to_all(
        outgoing(carried, send_fwd, group_count, group_width),
        "ctx",
        split_axis=1,
        concat_axis=1,
        tiled=True,
    )
    far_state = incoming(received, source_fwd, valid_fwd)
    received_back = lax.all_to_all(
        outgoing(back_carried, send_bwd, group_count, group_width),
        "ctx",
        split_axis=1,
        concat_axis=1,
        tiled=True,
    )
    near_state = incoming(received_back, source_bwd, valid_bwd)
    truncated = carried - band_tail * far_state
    layer_out = (skip_gain[None, :] * values + residue[None, :] * truncated).astype(jnp.bfloat16)
    back_truncated = back_carried - band_tail * near_state
    input_grad = (skip_gain[None, :] * upstream + residue[None, :] * back_truncated).astype(
        jnp.bfloat16
    )
    position = ctx_rank.astype(jnp.float32) * block_rows + offsets
    weighted = upstream * truncated
    moment = jnp.sum(position * weighted, axis=0) - jnp.sum(
        position * values * back_truncated, axis=0
    )
    grad_terms = jnp.stack(
        [jnp.sum(values * upstream, axis=0), jnp.sum(weighted, axis=0), -decay * residue * moment]
    )
    share_width = channels // lax.axis_size("ctx")
    summed = lax.psum(grad_terms, "ctx")
    own_share = lax.dynamic_slice_in_dim(summed, ctx_rank * share_width, share_width, 1)
    return (layer_out, input_grad, own_share[0], own_share[1], own_share[2])


MESH = pl.DeviceIdType.MESH
LANES = 128
ROWS = 8
PAIR = 2 * ROWS
PIECES = 4
UNROLL = 4


def greet(count, me):
    barrier = pltpu.get_barrier_semaphore()
    for step in range(1, count):
        pl.semaphore_signal(
            barrier,
            inc=1,
            device_id={"ctx": lax.rem(me + step, count)},
            device_id_type=MESH,
        )
    return lambda: pl.semaphore_wait(barrier, count - 1)


def pieces_of(count, slot):
    return PIECES if slot == count - 2 else 1


def pair_at(step):
    return pl.ds(pl.multiple_of(step * PAIR, PAIR), PAIR)


def banded_kernel(
    count,
    bands,
    x_hbm,
    c_hbm,
    residue_ref,
    decay_ref,
    skip_ref,
    out_hbm,
    grad_hbm,
    total_ref,
    x_all,
    c_all,
    xs,
    cs,
    far_x,
    far_c,
    ends,
    far_ends,
    outs,
    grads,
    sums,
    got,
    load_sem,
    store_sem,
    x_send,
    x_recv,
    c_send,
    c_recv,
    e_send,
    e_recv,
    s_send,
    s_recv,
):
    me = lax.axis_index("ctx")
    _, rows, width = x_all.shape
    shape = (ROWS, width)
    steps = rows // PAIR

    def load(source, target, at, group):
        lanes = pl.ds(group * width, width)
        return pltpu.make_async_copy(
            source.at[:, lanes], target.at[group], load_sem.at[at, group]
        )

    for at, (source, target) in enumerate(((x_hbm, x_all), (c_hbm, c_all))):
        for group in range(count):
            load(source, target, at, group).start()
    all_here = greet(count, me)
    groups = []
    for slot in range(count):
        group = jnp.int32(0)
        for other in range(count):
            group = jnp.where(bands[other] == slot, other, group)
        groups.append(group)

    def pack(whole, packed):
        def turn(step, _):
            at = pair_at(step)
            for slot in range(count):
                packed[slot, at, :] = whole[groups[slot], at, :]
            return 0

        lax.fori_loop(0, steps, turn, 0, unroll=UNROLL)

    for at, (source, target, packed) in enumerate(((x_hbm, x_all, xs), (c_hbm, c_all, cs))):
        for group in range(count):
            load(source, target, at, group).wait()
        pack(target, packed)

    first_sem = [sum(pieces_of(count, s) for s in range(slot)) for slot in range(count)]

    def x_copy(slot, piece):
        size = rows // pieces_of(count, slot)
        at = pl.ds(piece * size, size)
        sem = first_sem[slot] + piece
        return pltpu.make_async_remote_copy(
            src_ref=xs.at[slot, at],
            dst_ref=far_x.at[slot, at],
            send_sem=x_send.at[sem],
            recv_sem=x_recv.at[sem],
            device_id={"ctx": lax.rem(me + slot + 1, count)},
            device_id_type=MESH,
        )

    def c_copy(slot, piece):
        size = rows // pieces_of(count, slot)
        at = pl.ds(rows - (piece + 1) * size, size)
        sem = first_sem[slot] + piece
        return pltpu.make_async_remote_copy(
            src_ref=cs.at[slot, at],
            dst_ref=far_c.at[slot, at],
            send_sem=c_send.at[sem],
            recv_sem=c_recv.at[sem],
            device_id={"ctx": lax.rem(me + count - slot - 1, count)},
            device_id_type=MESH,
        )

    def small_copy(source, target, send, recv, step):
        return pltpu.make_async_remote_copy(
            src_ref=source,
            dst_ref=target,
            send_sem=send.at[step],
            recv_sem=recv.at[step],
            device_id={"ctx": lax.rem(me + step + 1, count)},
            device_id_type=MESH,
        )

    def end_copy(step):
        return small_copy(ends, far_ends.at[me], e_send, e_recv, step)

    def share_copy(slot, step):
        at = slot * (count - 1) + step
        return pltpu.make_async_remote_copy(
            src_ref=sums.at[slot],
            dst_ref=got.at[step, slot],
            send_sem=s_send.at[at],
            recv_sem=s_recv.at[at],
            device_id={"ctx": lax.rem(me + step + 1, count)},
            device_id_type=MESH,
        )

    def store(slot, piece, backward):
        pieces = pieces_of(count, slot)
        size = rows // pieces
        source, target = (grads, grad_hbm) if backward else (outs, out_hbm)
        at = pl.ds(rows - (piece + 1) * size if backward else piece * size, size)
        sem = store_sem.at[int(backward), first_sem[slot] + piece]
        return pltpu.make_async_copy(source.at[slot, at], target.at[slot, at], sem)

    def send(slot):
        for piece in range(pieces_of(count, slot)):
            pl.when(me + slot + 1 < count)(lambda: x_copy(slot, piece).start())
            pl.when(me >= slot + 1)(lambda: c_copy(slot, piece).start())

    all_here()
    send(0)

    level = lax.broadcasted_iota(jnp.int32, shape, 0)
    depth = level.astype(jnp.float32)
    zero = jnp.zeros(shape, jnp.float32)
    for slot in range(count):
        rate = decay_ref[groups[slot]]
        leap_pair = jnp.broadcast_to(jnp.exp(-rate * PAIR), shape)

        def turn(step, held):
            ahead = xs[slot, pair_at(step), :].astype(jnp.float32)
            back = cs[slot, pair_at(steps - 1 - step), :].astype(jnp.float32)
            parts = (ahead[:ROWS], ahead[ROWS:], back[:ROWS], back[ROWS:])
            return tuple(old * leap_pair + new for old, new in zip(held, parts))

        upper, lower, back_upper, back_lower = lax.fori_loop(
            0, steps, turn, (zero,) * 4, unroll=UNROLL
        )
        last = upper * jnp.exp(-rate * (PAIR - 1 - depth)) + lower * jnp.exp(
            -rate * (ROWS - 1 - depth)
        )
        first = back_upper * jnp.exp(-rate * depth) + back_lower * jnp.exp(
            -rate * (ROWS + depth)
        )
        ends[slot, 0:1, :] = jnp.sum(last, axis=0, keepdims=True)
        ends[slot, 1:2, :] = jnp.sum(first, axis=0, keepdims=True)
    for step in range(count - 1):
        end_copy(step).start()
    for slot in range(1, count - 1):
        send(slot)
    for step in range(count - 1):
        end_copy(step).wait()

    def scan(tile, hops):
        for hop, factor in hops:
            tile = tile + factor * pltpu.roll(tile, hop, 0)
        return tile

    def work(slot):
        band = slot + 1
        has_before = me >= band
        has_after = me + band < count
        reach = slot < count - 1
        rate = decay_ref[groups[slot]]
        residue_row = residue_ref[groups[slot]]
        carry = jnp.zeros((1, width), jnp.float32)
        back_carry = carry
        for other in range(count):
            apart = me - 1 - other
            kept = jnp.logical_and(apart >= 0, apart < band)
            factor = jnp.exp(-rate * (jnp.maximum(apart, 0) * rows).astype(jnp.float32))
            carry = carry + jnp.where(kept, factor * far_ends[other, slot, 0:1, :], 0.0)
            apart = other - me - 1
            kept = jnp.logical_and(apart >= 0, apart < band)
            factor = jnp.exp(-rate * (jnp.maximum(apart, 0) * rows).astype(jnp.float32))
            back_carry = back_carry + jnp.where(
                kept, factor * far_ends[other, slot, 1:2, :], 0.0
            )
        tail = jnp.broadcast_to(jnp.exp(-rate * float(band * rows)), shape)
        leap = jnp.broadcast_to(jnp.exp(-rate * ROWS), shape)
        residue = jnp.broadcast_to(residue_row, shape)
        skip = jnp.broadcast_to(skip_ref[groups[slot]], shape)
        lead = jnp.exp(-rate * (depth + 1.0))
        trail = jnp.exp(-rate * (ROWS - depth))
        fwd = [
            (hop, jnp.where(level >= hop, jnp.exp(-rate * hop), 0.0)) for hop in (1, 2, 4)
        ]
        bwd = [
            (ROWS - hop, jnp.where(level < ROWS - hop, jnp.exp(-rate * hop), 0.0))
            for hop in (1, 2, 4)
        ]

        def forward(step, state):
            carry, s_skip, s_w, s_tw = state
            at = pair_at(step)
            base = (step * PAIR).astype(jnp.float32)
            x = xs[slot, at, :].astype(jnp.float32)
            c = cs[slot, at, :].astype(jnp.float32)
            if reach:
                far = far_x[slot, at, :].astype(jnp.float32)
            made = []
            for half in range(2):
                part = slice(half * ROWS, (half + 1) * ROWS)
                fresh = x[part]
                if reach:
                    fresh = fresh - jnp.where(has_before, tail * far[part], 0.0)
                local = scan(fresh, fwd)
                truncated = local + lead * carry
                carry = leap * carry + jnp.broadcast_to(local[ROWS - 1 :], shape)
                made.append(skip * x[part] + residue * truncated)
                w = c[part] * truncated
                s_skip = s_skip + x[part] * c[part]
                s_w = s_w + w
                s_tw = s_tw + (base + half * ROWS) * w
            outs[slot, at, :] = jnp.concatenate(made, axis=0).astype(outs.dtype)
            return carry, s_skip, s_w, s_tw

        def backward(step, state):
            carry, unused, s_v, s_tv = state
            at = pair_at(steps - 1 - step)
            base = ((steps - 1 - step) * PAIR).astype(jnp.float32)
            x = xs[slot, at, :].astype(jnp.float32)
            c = cs[slot, at, :].astype(jnp.float32)
            if reach:
                far = far_c[slot, at, :].astype(jnp.float32)
            made = [None, None]
            for half in (1, 0):
                part = slice(half * ROWS, (half + 1) * ROWS)
                fresh = c[part]
                if reach:
                    fresh = fresh - jnp.where(has_after, tail * far[part], 0.0)
                local = scan(fresh, bwd)
                truncated = local + trail * carry
                carry = leap * carry + jnp.broadcast_to(local[:1], shape)
                made[half] = skip * c[part] + residue * truncated
                v = x[part] * truncated
                s_v = s_v + v
                s_tv = s_tv + (base + half * ROWS) * v
            grads[slot, at, :] = jnp.concatenate(made, axis=0).astype(grads.dtype)
            return carry, unused, s_v, s_tv

        ahead = (jnp.broadcast_to(carry, shape), zero, zero, zero)
        back = (jnp.broadcast_to(back_carry, shape), zero, zero, zero)
        pieces = pieces_of(count, slot)

        def run(backwards, state):
            for piece in range(pieces):
                span = (piece * steps // pieces, (piece + 1) * steps // pieces)
                if reach and backwards:
                    pl.when(has_after)(lambda: c_copy(slot, piece).wait_recv())
                elif reach:
                    pl.when(has_before)(lambda: x_copy(slot, piece).wait_recv())
                turn = backward if backwards else forward
                state = lax.fori_loop(*span, turn, state, unroll=UNROLL)
                store(slot, piece, backwards).start()
            return state

        if not reach or 2 * band < count:
            ahead = run(False, ahead)
            back = run(True, back)
            close(slot, rate, residue_row, ahead, back)
            return None
        ready = lax.cond(has_after, lambda: run(False, ahead), lambda: run(True, back))

        def rest():
            late = lax.cond(has_after, lambda: run(True, back), lambda: run(False, ahead))
            pick = lambda left, right: tuple(
                jnp.where(has_after, one, two) for one, two in zip(left, right)
            )
            close(slot, rate, residue_row, pick(ready, late), pick(late, ready))

        return rest

    def close(slot, rate, residue_row, ahead, back):
        _, s_skip, s_w, s_tw = ahead
        _, _, s_v, s_tv = back
        offset = depth + (me * rows).astype(jnp.float32)
        moment = (s_tw - s_tv) + offset * (s_w - s_v)
        sums[slot, 0:1, :] = jnp.sum(s_skip, axis=0, keepdims=True)
        sums[slot, 1:2, :] = jnp.sum(s_w, axis=0, keepdims=True)
        sums[slot, 2:3, :] = (
            -rate * residue_row * jnp.sum(moment, axis=0, keepdims=True)
        )
        for step in range(count - 1):
            share_copy(slot, step).start()

    sums[...] = jnp.zeros_like(sums)
    work(count - 1)
    pending = [work(slot) for slot in range(count - 1)]
    for rest in pending:
        if rest is not None:
            rest()

    for slot in range(count):
        for piece in range(pieces_of(count, slot)):
            store(slot, piece, False).wait()
            store(slot, piece, True).wait()
    for slot in range(count):
        total = sums[slot]
        for step in range(count - 1):
            share_copy(slot, step).wait()
            total = total + got[step, slot]
        total_ref[slot] = total
    for slot in range(count - 1):
        for piece in range(pieces_of(count, slot)):
            pl.when(me + slot + 1 < count)(lambda: x_copy(slot, piece).wait_send())
            pl.when(me >= slot + 1)(lambda: c_copy(slot, piece).wait_send())


def place_kernel(bands, out, grad, total, out_ref, grad_ref, skip_ref, residue_ref, decay_ref):
    out_ref[...] = out[0]
    grad_ref[...] = grad[0]
    own = total[bands[lax.axis_index("ctx")]]
    skip_ref[...] = own[0:1]
    residue_ref[...] = own[1:2]
    decay_ref[...] = own[2:3]


def place(bands, outs, grads, totals):
    count, rows, width = outs.shape
    slot = pl.BlockSpec((1, rows, width), lambda g, r, bands: (bands[g], r, 0))
    block = pl.BlockSpec((rows, width), lambda g, r, bands: (r, g))
    one = pl.BlockSpec((1, width), lambda g, r, bands: (0, 0))
    whole = jax.ShapeDtypeStruct((rows, count * width), outs.dtype)
    small = jax.ShapeDtypeStruct((1, width), totals.dtype)
    return pl.pallas_call(
        place_kernel,
        grid_spec=pltpu.PrefetchScalarGridSpec(
            num_scalar_prefetch=1,
            grid=(count, 1),
            in_specs=[
                slot,
                slot,
                pl.BlockSpec(totals.shape, lambda g, r, bands: (0, 0, 0)),
            ],
            out_specs=[block, block, one, one, one],
        ),
        out_shape=(whole, whole, small, small, small),
        name="place",
    )(bands, outs, grads, totals)


def banded(count, inputs, cotangent, residue, decay, skip_gain, band_blocks):
    rows, channels = inputs.shape
    width = channels // count
    bands = band_blocks[0]
    anywhere = pl.BlockSpec(memory_space=pl.ANY)
    inside = pl.BlockSpec(memory_space=pltpu.VMEM)
    flows = sum(pieces_of(count, slot) for slot in range(count))
    many = pltpu.SemaphoreType.DMA((flows,))
    few = pltpu.SemaphoreType.DMA((count - 1,))
    some = pltpu.SemaphoreType.DMA((count * (count - 1),))
    packed = pltpu.VMEM((count, rows, width), inputs.dtype)
    far = pltpu.VMEM((count - 1, rows, width), inputs.dtype)
    outs, grads, totals = pl.pallas_call(
        functools.partial(banded_kernel, count),
        in_specs=[
            pl.BlockSpec(memory_space=pltpu.SMEM),
            anywhere,
            anywhere,
            inside,
            inside,
            inside,
        ],
        out_specs=[anywhere, anywhere, inside],
        out_shape=(
            jax.ShapeDtypeStruct((count, rows, width), inputs.dtype),
            jax.ShapeDtypeStruct((count, rows, width), inputs.dtype),
            jax.ShapeDtypeStruct((count, ROWS // 2, width), jnp.float32),
        ),
        scratch_shapes=[
            packed,
            packed,
            packed,
            packed,
            far,
            far,
            pltpu.VMEM((count, 2, width), jnp.float32),
            pltpu.VMEM((count, count, 2, width), jnp.float32),
            packed,
            packed,
            pltpu.VMEM((count, ROWS // 2, width), jnp.float32),
            pltpu.VMEM((count - 1, count, ROWS // 2, width), jnp.float32),
            pltpu.SemaphoreType.DMA((2, count)),
            pltpu.SemaphoreType.DMA((2, flows)),
            many,
            many,
            many,
            many,
            few,
            few,
            some,
            some,
        ],
        compiler_params=pltpu.CompilerParams(collective_id=0, has_side_effects=True),
        name="banded",
    )(
        bands,
        inputs,
        cotangent,
        *(part.reshape(count, 1, width) for part in (residue, decay, skip_gain)),
    )
    layer_out, input_grad, *sums = place(bands, outs, grads, totals)
    return (layer_out, input_grad, *(part.reshape(width) for part in sums))


def local_body(count, inputs, cotangent, residue, decay, skip_gain, band_blocks):
    rows, channels = inputs.shape
    groups = band_blocks.shape[1]
    fits = groups == count and count > 1 and rows % (PAIR * PIECES) == 0
    if fits and channels % (groups * LANES) == 0:
        return banded(count, inputs, cotangent, residue, decay, skip_gain, band_blocks)
    return body(inputs, cotangent, residue, decay, skip_gain, band_blocks)


def solution(mesh):
    placed = (P("ctx", "dp"), P("ctx", "dp"), P("dp"), P("dp"), P("dp"), P("dp", None))
    return jax.shard_map(
        functools.partial(local_body, mesh.shape["ctx"]),
        mesh=mesh,
        in_specs=placed,
        out_specs=(
            P("ctx", "dp"),
            P("ctx", "dp"),
            P(("dp", "ctx")),
            P(("dp", "ctx")),
            P(("dp", "ctx")),
        ),
        check_vma=False,
    )
```
